32 devices in a mesh: parts: 2 (over y), seq: 4 (over z), heads: 2 (over x), sub: 2 (over core).
Axes of the slice: x: 2, y: 2, z: 4, core: 2. Of those that a mesh axis runs over, the one named last changes fastest.
Arguments:
- queries: bfloat16 [8192, 4096], P(('parts', 'seq', 'sub'), 'heads'), parts along dimension 0, as said below
- keys: bfloat16 [8192, 4096], P(('parts', 'seq', 'sub'), 'heads'), parts along dimension 0, as said below
- values: bfloat16 [8192, 4096], P(('parts', 'seq', 'sub'), 'heads'), parts along dimension 0, may hold values from -6 to 6
- half_width: int32 [32], replicated, may hold values from 128 to 512, as said below
- valid_length: int32 [2], P('parts'), parts along dimension 0, may hold values from 3328 to 4096
- out_weight: bfloat16 [4096, 4096], P('heads', 'sub'), may hold values from -1.5 to 1.5
Outputs:
- projected: bfloat16 [8192, 4096], P(('parts', 'seq', 'sub'), 'heads'), parts along dimension 0
The draws below stay inside these ranges and needn't reach their ends.
There are 2 independent parts, one for each index of `parts`. The reference program is written for one: setup_inputs(seed, part) draws one part's arguments, and reference() takes and returns one part's arrays. A program takes and returns all parts, laid end to end along the dimension named above; an argument that names none is the same for every part. Nothing has to cross between parts.
Inputs may be any that keep to these rules, and one draw needn't show every extreme that they name: queries with 32 heads of 128 entries side by side. keys with 32 heads of 128 entries side by side. `half_width`: some head's half-width is exactly 512.
All inputs are finite; a program needn't handle non-finite values.
Results may differ from the reference program's by a relative error of at most 0.014.
Values may be sent and summed in bfloat16 or wider, within the bound.
A program may use at most 192 MiB of HBM per device.

```python
import math
import jax
import jax.numpy as jnp
from jax import lax

H = 32
HD = 128
D = 4096
TOK_DEV = 512
TOKENS = 4096
N_HEADS = 2


def common_draw(key):
    total_width = H * HD
    query_raw = jax.random.normal(jax.random.fold_in(key, 11), (TOKENS, total_width), jnp.float32)
    key_raw = jax.random.normal(jax.random.fold_in(key, 12), (TOKENS, total_width), jnp.float32)
    return (query_raw, key_raw)


def draw_queries(key, part):
    return common_draw(key)[0].astype(jnp.bfloat16)


def draw_keys(key, part):
    return common_draw(key)[1].astype(jnp.bfloat16)


def draw_half_width(key, part):
    widths = jax.random.randint(jax.random.fold_in(key, 21), (H,), TOK_DEV // 4, TOK_DEV + 1).astype(jnp.int32)
    order = jax.random.permutation(jax.random.fold_in(key, 22), H)
    widths = widths.at[order[0]].set(TOK_DEV)
    widths = widths.at[order[1]].set(TOK_DEV // 4)
    return widths.astype(jnp.int32)


def with_spikes(array, own_key, source, target, shards_of, factor):
    owner, partner = [(jnp.arange(array.shape[position]) // (array.shape[position] // shards_of)).reshape([-1 if axis == position else 1 for axis in range(array.ndim)]) for position in (source, target)]
    chosen = jax.random.permutation(own_key, shards_of)[partner]
    strong = (owner == chosen) | (owner == (partner + shards_of // 2) % shards_of)
    return jnp.where(strong, factor * array, array)


def block_levels(rng, dims, cuts, least, high):
    def one(axis_at, blocks):
        heights = jax.random.uniform(jax.random.fold_in(jax.random.fold_in(rng, 6), axis_at), (blocks,), jnp.float32, least / len(cuts), high / len(cuts))
        return jnp.repeat(jnp.exp(heights), dims[axis_at] // blocks).reshape((-1,) + (1,) * (len(dims) - axis_at - 1))

    gain = one(*cuts[0])
    for cut in cuts[1:]:
        gain = gain * one(*cut)
    return gain


def normal_values(rng, shape, spread, most, cuts=(), kind=jnp.bfloat16):
    drawn = jax.random.normal(rng, shape, jnp.float32) * spread
    if len(cuts) > 0:
        drawn = block_levels(rng, shape, cuts, -0.22, 0.18) * drawn
    return jnp.clip(drawn, min=-most, max=most).astype(kind)


def gaussian_with(stream_key, dims, spread, reach, shards, heavy, held_as=jnp.bfloat16):
    array = spread * jax.random.normal(stream_key, dims, jnp.float32)
    if shards:
        array = array * block_levels(stream_key, dims, shards, -0.22, 0.18)
    return jnp.clip(with_spikes(array, jax.random.fold_in(stream_key, 3), *heavy), -reach, reach).astype(held_as)


def setup_inputs(seed: int = 0, part: int = 0) -> dict:
    splits = jax.random.split(jax.random.key(seed), 7)
    own_keys = jax.random.split(jax.random.fold_in(splits[6], part), 7)
    return {
        "queries": draw_queries(jax.random.fold_in(jax.random.fold_in(splits[6], part), 71), part),
        "keys": draw_keys(jax.random.fold_in(jax.random.fold_in(splits[6], part), 71), part),
        "values": normal_values(own_keys[2], (TOKENS, H * HD), 1.0, 6.0, ((0, 8), (1, 2))),
        "half_width": draw_half_width(jax.random.fold_in(splits[6], 71), part),
        "valid_length": jax.random.randint(own_keys[4], (1,), TOKENS - TOK_DEV - TOK_DEV // 2, TOKENS + 1).astype(jnp.int32),
        "out_weight": gaussian_with(splits[5], (H * HD, D), H ** -0.5, 1.5, ((0, 2), (1, 2)), (0, 1, 2, 2.0)),
    }


def reference(queries, keys, values, half_width, valid_length, out_weight):
    heads_group = H // N_HEADS
    query_heads = queries.reshape(TOKENS, H, HD)
    key_heads = keys.reshape(TOKENS, H, HD)
    value_heads = values.reshape(TOKENS, H, HD)
    padding = jnp.zeros((TOK_DEV, H, HD), jnp.bfloat16)
    key_padded = jnp.concatenate([padding, key_heads, padding], axis=0)
    value_padded = jnp.concatenate([padding, value_heads, padding], axis=0)
    length_end = valid_length[0]
    score_scale = 1.0 / math.sqrt(HD)
    block_count = TOKENS // TOK_DEV

    def one_block(block_index):
        first_row = block_index * TOK_DEV
        query_block = lax.dynamic_slice_in_dim(query_heads, first_row, TOK_DEV, 0)
        key_block = lax.dynamic_slice_in_dim(key_padded, first_row, 3 * TOK_DEV, 0)
        value_block = lax.dynamic_slice_in_dim(value_padded, first_row, 3 * TOK_DEV, 0)
        query_pos = first_row + jnp.arange(TOK_DEV, dtype=jnp.int32)
        key_pos = first_row - TOK_DEV + jnp.arange(3 * TOK_DEV, dtype=jnp.int32)
        distance = jnp.abs(query_pos[:, None] - key_pos[None, :])
        key_fine = (key_pos >= 0) & (key_pos < length_end)
        opened = (distance[None, :, :] <= half_width[:, None, None]) & key_fine[None, None, :]
        scores = jnp.einsum('ihd,jhd->hij', query_block.astype(jnp.float32), key_block.astype(jnp.float32)) * score_scale
        highest = lax.optimization_barrier(jnp.max(jnp.where(opened, scores, jnp.float32(-1e+30)), axis=2, keepdims=True))
        weights = jnp.where(opened, jnp.exp(scores - highest), jnp.float32(0.0))
        totals = lax.optimization_barrier(jnp.sum(weights, axis=2))
        weights_low = lax.optimization_barrier(weights.astype(jnp.bfloat16))
        numerator = jnp.einsum('hij,jhd->ihd', weights_low.astype(jnp.float32), value_block.astype(jnp.float32))
        valid_rows = query_pos < length_end
        safe_totals = jnp.where(valid_rows[None, :], totals, jnp.float32(1.0))
        attended_block = numerator / safe_totals.T[:, :, None]
        attended_block = jnp.where(valid_rows[:, None, None], attended_block, jnp.float32(0.0))
        return attended_block.reshape(TOK_DEV, H * HD).astype(jnp.bfloat16)
    attended = lax.map(one_block, jnp.arange(block_count, dtype=jnp.int32)).reshape(TOKENS, H * HD)
    group_width = heads_group * HD

    def add_group(running, group_index):
        columns = lax.dynamic_slice_in_dim(attended, group_index * group_width, group_width, 1)
        weight_rows = lax.dynamic_slice_in_dim(out_weight, group_index * group_width, group_width, 0)
        group_sum = jnp.dot(columns, weight_rows, preferred_element_type=jnp.float32).astype(jnp.bfloat16)
        group_sum = lax.optimization_barrier(group_sum)
        return (running + group_sum.astype(jnp.float32), None)
    summed, unused = lax.scan(add_group, jnp.zeros((TOKENS, D), jnp.float32), jnp.arange(H // heads_group, dtype=jnp.int32))
    return summed.astype(jnp.bfloat16)
```

```python
import functools
import math

import jax
import jax.numpy as jnp
from jax import lax
from jax.experimental import pallas as pl
from jax.experimental.pallas import tpu as pltpu
from jax.sharding import PartitionSpec as P

HD = 128
STEPS = 4
PARTS = 4
CLOSED = -1e30
FAR = 1 << 20
EXP2_SCALE = math.log2(math.e) / math.sqrt(HD)
MESH = pl.DeviceIdType.MESH


def kernel(
    half_width,
    valid_length,
    q_hbm,
    k_hbm,
    v_hbm,
    w_hbm,
    out_ref,
    qbuf,
    kbuf,
    vbuf,
    wbuf,
    distance,
    attended,
    own_terms,
    x_out,
    x_in,
    local_sem,
    z_send,
    z_recv,
    c_send,
    c_recv,
    w_send,
    w_recv,
    x_send,
    x_recv,
):
    rows, width = qbuf.shape
    heads_here = width // HD
    chunk = rows // STEPS
    span = 2 * rows + chunk
    cols = width // PARTS
    seq = lax.axis_index("seq")
    group = lax.axis_index("heads")
    sub = lax.axis_index("sub")
    has_z = jnp.where(sub == 0, seq > 0, seq < lax.axis_size("seq") - 1)
    chip_peer = {"sub": 1 - sub}
    z_peer = {"seq": seq + 2 * sub - 1, "sub": 1 - sub}
    x_peer = {"heads": 1 - group}
    first = (seq * 2 + sub) * rows
    length_end = valid_length[0]

    barrier = pltpu.get_barrier_semaphore()
    pl.semaphore_signal(barrier, inc=1, device_id=chip_peer, device_id_type=MESH)
    pl.semaphore_signal(barrier, inc=1, device_id=x_peer, device_id_type=MESH)

    @pl.when(has_z)
    def _():
        pl.semaphore_signal(barrier, inc=1, device_id=z_peer, device_id_type=MESH)

    own_rows = pl.ds(rows, rows)
    locals_ = [
        pltpu.make_async_copy(q_hbm, qbuf, local_sem.at[0]),
        pltpu.make_async_copy(k_hbm, kbuf.at[own_rows], local_sem.at[1]),
        pltpu.make_async_copy(v_hbm, vbuf.at[own_rows], local_sem.at[2]),
        pltpu.make_async_copy(w_hbm, wbuf.at[sub], local_sem.at[3]),
    ]
    for copy in locals_[:3]:
        copy.start()
    pl.semaphore_wait(barrier, 2 + has_z.astype(jnp.int32))

    def z_copies(step, sender):
        source = jnp.where(sender == 0, step, STEPS - 1 - step) * chunk
        landing = source + jnp.where(sender == 0, 2 * rows, 0)
        source = pl.ds(pl.multiple_of(source, chunk), chunk)
        landing = pl.ds(pl.multiple_of(landing, chunk), chunk)
        return [
            pltpu.make_async_remote_copy(
                src_ref=hbm.at[source],
                dst_ref=buf.at[landing],
                send_sem=z_send.at[which, step],
                recv_sem=z_recv.at[which, step],
                device_id=z_peer,
                device_id_type=MESH,
            )
            for which, (hbm, buf) in enumerate(((k_hbm, kbuf), (v_hbm, vbuf)))
        ]

    def c_copies(sender):
        landing = pl.ds(pl.multiple_of(jnp.where(sender == 0, 0, 2 * rows), chunk), rows)
        return [
            pltpu.make_async_remote_copy(
                src_ref=hbm,
                dst_ref=buf.at[landing],
                send_sem=c_send.at[which],
                recv_sem=c_recv.at[which],
                device_id=chip_peer,
                device_id_type=MESH,
            )
            for which, (hbm, buf) in enumerate(((k_hbm, kbuf), (v_hbm, vbuf)))
        ]

    def w_copy(sender):
        return pltpu.make_async_remote_copy(
            src_ref=w_hbm,
            dst_ref=wbuf.at[sender],
            send_sem=w_send,
            recv_sem=w_recv,
            device_id=chip_peer,
            device_id_type=MESH,
        )

    def query_rows(step):
        return pl.multiple_of(jnp.where(sub == 0, STEPS - 1 - step, step) * chunk, chunk)

    def x_copy(step, part):
        here = (pl.ds(query_rows(step), chunk), pl.ds(part * cols, cols))
        return pltpu.make_async_remote_copy(
            src_ref=x_out.at[here],
            dst_ref=x_in.at[here],
            send_sem=x_send.at[step, part],
            recv_sem=x_recv.at[step, part],
            device_id=x_peer,
            device_id_type=MESH,
        )

    @pl.when(has_z)
    def _():
        for copy in z_copies(0, sub):
            copy.start()

    for copy in c_copies(sub):
        copy.start()

    @pl.when(has_z)
    def _():
        for step in range(1, STEPS):
            for copy in z_copies(step, sub):
                copy.start()

    w_copy(sub).start()
    locals_[3].start()

    @pl.when(jnp.logical_not(has_z))
    def _():
        edge = pl.ds(pl.multiple_of(jnp.where(sub == 0, 0, 2 * rows), chunk), rows)
        kbuf[edge, :] = jnp.zeros((rows, width), kbuf.dtype)
        vbuf[edge, :] = jnp.zeros((rows, width), vbuf.dtype)

    for copy in locals_[:3]:
        copy.wait()
    for copy in c_copies(1 - sub):
        copy.wait_recv()

    def finish(step):
        for part in range(PARTS):
            x_copy(step, part).wait_recv()
        here = pl.ds(query_rows(step), chunk)
        out_ref[here, :] = (own_terms[here, :] + x_in[here, :].astype(jnp.float32)).astype(
            out_ref.dtype
        )

    def one_step(step, carry):
        row = query_rows(step)
        queries_here = pl.ds(row, chunk)
        keys_here = pl.ds(row, span)

        @pl.when(has_z)
        def _():
            for copy in z_copies(step, 1 - sub):
                copy.wait_recv()

        row_at = lax.broadcasted_iota(jnp.int32, (chunk, span), 0)
        key_at = lax.broadcasted_iota(jnp.int32, (chunk, span), 1)
        key_pos = key_at + (first + row - rows)
        distance[...] = jnp.where(
            (key_pos >= 0) & (key_pos < length_end), jnp.abs(row_at + rows - key_at), FAR
        )
        row_fine = (
            lax.broadcasted_iota(jnp.int32, (chunk, HD), 0) + (first + row)
        ) < length_end

        def one_head(head, carry):
            lanes = pl.ds(pl.multiple_of(head * HD, HD), HD)
            scores = lax.dot_general(
                qbuf[queries_here, lanes],
                kbuf[keys_here, lanes],
                (((1,), (1,)), ((), ())),
                preferred_element_type=jnp.float32,
            )
            scores = jnp.where(
                distance[...] <= half_width[group * heads_here + head], scores, CLOSED
            )
            top = jnp.max(scores, axis=1, keepdims=True)
            weights = jnp.exp2((scores - top) * EXP2_SCALE)
            total = jnp.sum(weights, axis=1, keepdims=True)
            sums = jnp.dot(
                weights.astype(jnp.bfloat16),
                vbuf[keys_here, lanes],
                preferred_element_type=jnp.float32,
            )
            attended[:, lanes] = jnp.where(row_fine, sums / total, 0.0).astype(attended.dtype)
            return carry

        lax.fori_loop(0, heads_here, one_head, 0, unroll=2)

        @pl.when(step == 0)
        def _():
            locals_[3].wait()
            w_copy(1 - sub).wait_recv()

        for part in range(2 * PARTS):
            at = pl.ds((part % PARTS) * cols, cols)
            block = 1 - group if part < PARTS else group
            terms = jnp.dot(
                attended[...], wbuf[block, :, at], preferred_element_type=jnp.float32
            )
            if part < PARTS:
                x_out[queries_here, at] = terms.astype(x_out.dtype)
            else:
                own_terms[queries_here, at] = terms
            if 1 <= part <= PARTS:
                x_copy(step, part - 1).start()

        @pl.when(step > 0)
        def _():
            finish(step - 1)

        return carry

    lax.fori_loop(0, STEPS, one_step, 0)
    finish(STEPS - 1)

    for step in range(STEPS):
        for part in range(PARTS):
            x_copy(step, part).wait_send()
    for copy in c_copies(sub):
        copy.wait_send()
    w_copy(sub).wait_send()

    @pl.when(has_z)
    def _():
        for step in range(STEPS):
            for copy in z_copies(step, sub):
                copy.wait_send()


def local(queries, keys, values, half_width, valid_length, out_weight):
    rows, width = queries.shape
    chunk = rows // STEPS
    bf16 = jnp.bfloat16
    dma = pltpu.SemaphoreType.DMA
    return pl.pallas_call(
        kernel,
        out_shape=jax.ShapeDtypeStruct((rows, width), bf16),
        in_specs=[pl.BlockSpec(memory_space=pltpu.SMEM)] * 2
        + [pl.BlockSpec(memory_space=pl.ANY)] * 4,
        out_specs=pl.BlockSpec(memory_space=pltpu.VMEM),
        scratch_shapes=[
            pltpu.VMEM((rows, width), bf16),
            pltpu.VMEM((3 * rows, width), bf16),
            pltpu.VMEM((3 * rows, width), bf16),
            pltpu.VMEM((2,) + out_weight.shape, bf16),
            pltpu.VMEM((chunk, 2 * rows + chunk), jnp.int32),
            pltpu.VMEM((chunk, width), bf16),
            pltpu.VMEM((rows, width), jnp.float32),
            pltpu.VMEM((rows, width), bf16),
            pltpu.VMEM((rows, width), bf16),
            dma((4,)),
            dma((2, STEPS)),
            dma((2, STEPS)),
            dma((2,)),
            dma((2,)),
            dma,
            dma,
            dma((STEPS, PARTS)),
            dma((STEPS, PARTS)),
        ],
        compiler_params=pltpu.CompilerParams(
            collective_id=0, has_side_effects=True, vmem_limit_bytes=60 << 20
        ),
    )(half_width, valid_length, queries, keys, values, out_weight)


def solution(mesh):
    placed = (
        P(("parts", "seq", "sub"), "heads"),
        P(("parts", "seq", "sub"), "heads"),
        P(("parts", "seq", "sub"), "heads"),
        P(),
        P("parts"),
        P("heads", "sub"),
    )
    return jax.shard_map(
        local,
        mesh=mesh,
        in_specs=placed,
        out_specs=P(("parts", "seq", "sub"), "heads"),
        check_vma=False,
    )
```

```python
import functools
import math

import jax
import jax.numpy as jnp
from jax import lax
from jax.experimental import pallas as pl
from jax.experimental.pallas import tpu as pltpu
from jax.sharding import PartitionSpec as P

HD = 128
LAYERS = (128, 128, 128, 128)
REACH = 128
STEPS = len(LAYERS)
STARTS = tuple(sum(LAYERS[:step]) for step in range(STEPS))
PARTS = 4
CLOSED = -1e30
FAR = 1 << 20
EXP2_SCALE = math.log2(math.e) / math.sqrt(HD)
MESH = pl.DeviceIdType.MESH


def kernel(
    half_width,
    valid_length,
    q_hbm,
    k_hbm,
    v_hbm,
    w_hbm,
    out_ref,
    qbuf,
    kbuf,
    vbuf,
    wbuf,
    distance,
    attended,
    own_terms,
    x_out,
    x_in,
    local_sem,
    z_send,
    z_recv,
    c_send,
    c_recv,
    w_send,
    w_recv,
    x_send,
    x_recv,
):
    rows, width = qbuf.shape
    heads_here = width // HD
    span = 2 * rows + REACH
    cols = width // PARTS
    seq = lax.axis_index("seq")
    group = lax.axis_index("heads")
    sub = lax.axis_index("sub")
    has_z = jnp.where(sub == 0, seq > 0, seq < lax.axis_size("seq") - 1)
    chip_peer = {"sub": 1 - sub}
    z_peer = {"seq": seq + 2 * sub - 1, "sub": 1 - sub}
    x_peer = {"heads": 1 - group}
    first = (seq * 2 + sub) * rows
    length_end = valid_length[0]

    barrier = pltpu.get_barrier_semaphore()
    pl.semaphore_signal(barrier, inc=1, device_id=chip_peer, device_id_type=MESH)
    pl.semaphore_signal(barrier, inc=1, device_id=x_peer, device_id_type=MESH)

    @pl.when(has_z)
    def _():
        pl.semaphore_signal(barrier, inc=1, device_id=z_peer, device_id_type=MESH)

    own_rows = pl.ds(rows, rows)
    locals_ = [
        pltpu.make_async_copy(q_hbm, qbuf, local_sem.at[0]),
        pltpu.make_async_copy(k_hbm, kbuf.at[own_rows], local_sem.at[1]),
        pltpu.make_async_copy(v_hbm, vbuf.at[own_rows], local_sem.at[2]),
        pltpu.make_async_copy(w_hbm, wbuf.at[sub], local_sem.at[3]),
    ]
    for copy in locals_[:3]:
        copy.start()
    pl.semaphore_wait(barrier, 2 + has_z.astype(jnp.int32))

    def z_copies(step, sender):
        start, size = STARTS[step], LAYERS[step]
        source = jnp.where(sender == 0, start, rows - size - start)
        landing = source + jnp.where(sender == 0, 2 * rows, 0)
        source = pl.ds(pl.multiple_of(source, 32), size)
        landing = pl.ds(pl.multiple_of(landing, 32), size)
        return [
            pltpu.make_async_remote_copy(
                src_ref=hbm.at[source],
                dst_ref=buf.at[landing],
                send_sem=z_send.at[which, step],
                recv_sem=z_recv.at[which, step],
                device_id=z_peer,
                device_id_type=MESH,
            )
            for which, (hbm, buf) in enumerate(((k_hbm, kbuf), (v_hbm, vbuf)))
        ]

    def c_copies(sender):
        landing = pl.ds(pl.multiple_of(jnp.where(sender == 0, 0, 2 * rows), rows), rows)
        return [
            pltpu.make_async_remote_copy(
                src_ref=hbm,
                dst_ref=buf.at[landing],
                send_sem=c_send.at[which],
                recv_sem=c_recv.at[which],
                device_id=chip_peer,
                device_id_type=MESH,
            )
            for which, (hbm, buf) in enumerate(((k_hbm, kbuf), (v_hbm, vbuf)))
        ]

    def w_copy(sender):
        return pltpu.make_async_remote_copy(
            src_ref=w_hbm,
            dst_ref=wbuf.at[sender],
            send_sem=w_send,
            recv_sem=w_recv,
            device_id=chip_peer,
            device_id_type=MESH,
        )

    def query_rows(step):
        start, size = STARTS[step], LAYERS[step]
        return pl.multiple_of(jnp.where(sub == 0, rows - size - start, start), 32)

    def x_copy(step, part):
        here = (pl.ds(query_rows(step), LAYERS[step]), pl.ds(part * cols, cols))
        return pltpu.make_async_remote_copy(
            src_ref=x_out.at[here],
            dst_ref=x_in.at[here],
            send_sem=x_send.at[step, part],
            recv_sem=x_recv.at[step, part],
            device_id=x_peer,
            device_id_type=MESH,
        )

    @pl.when(has_z)
    def _():
        for copy in z_copies(0, sub):
            copy.start()

    for copy in c_copies(sub):
        copy.start()

    @pl.when(has_z)
    def _():
        for step in range(1, STEPS):
            for copy in z_copies(step, sub):
                copy.start()

    w_copy(sub).start()
    locals_[3].start()

    @pl.when(jnp.logical_not(has_z))
    def _():
        edge = pl.ds(pl.multiple_of(jnp.where(sub == 0, 0, 2 * rows), rows), rows)
        kbuf[edge, :] = jnp.zeros((rows, width), kbuf.dtype)
        vbuf[edge, :] = jnp.zeros((rows, width), vbuf.dtype)

    for copy in locals_[:3]:
        copy.wait()
    for copy in c_copies(1 - sub):
        copy.wait_recv()

    def finish(step):
        for part in range(PARTS):
            x_copy(step, part).wait_recv()
        here = pl.ds(query_rows(step), LAYERS[step])
        out_ref[here, :] = (own_terms[here, :] + x_in[here, :].astype(jnp.float32)).astype(
            out_ref.dtype
        )

    def one_step(step):
        chunk = LAYERS[step]
        row = query_rows(step)
        lead = jnp.where(sub == 0, 0, REACH - chunk)
        queries_here = pl.ds(row, chunk)
        keys_here = pl.ds(pl.multiple_of(row - lead, 32), span)

        @pl.when(has_z)
        def _():
            for copy in z_copies(step, 1 - sub):
                copy.wait_recv()

        row_at = lax.broadcasted_iota(jnp.int32, (chunk, span), 0)
        key_at = lax.broadcasted_iota(jnp.int32, (chunk, span), 1)
        key_pos = key_at + (first + row - lead - rows)
        distance[:chunk, :] = jnp.where(
            (key_pos >= 0) & (key_pos < length_end), jnp.abs(row_at + (rows + lead) - key_at), FAR
        )
        row_fine = (
            lax.broadcasted_iota(jnp.int32, (chunk, HD), 0) + (first + row)
        ) < length_end

        def one_head(head, carry):
            lanes = pl.ds(pl.multiple_of(head * HD, HD), HD)
            scores = lax.dot_general(
                qbuf[queries_here, lanes],
                kbuf[keys_here, lanes],
                (((1,), (1,)), ((), ())),
                preferred_element_type=jnp.float32,
            )
            scores = jnp.where(
                distance[:chunk, :] <= half_width[group * heads_here + head], scores, CLOSED
            )
            top = jnp.max(scores, axis=1, keepdims=True)
            weights = jnp.exp2((scores - top) * EXP2_SCALE)
            total = jnp.sum(weights, axis=1, keepdims=True)
            sums = jnp.dot(
                weights.astype(jnp.bfloat16),
                vbuf[keys_here, lanes],
                preferred_element_type=jnp.float32,
            )
            attended[:chunk, lanes] = jnp.where(row_fine, sums / total, 0.0).astype(attended.dtype)
            return carry

        lax.fori_loop(0, heads_here, one_head, 0, unroll=4)

        if step == 0:
            locals_[3].wait()
            w_copy(1 - sub).wait_recv()

        for part in range(2 * PARTS):
            at = pl.ds((part % PARTS) * cols, cols)
            block = 1 - group if part < PARTS else group
            terms = jnp.dot(
                attended[:chunk, :], wbuf[block, :, at], preferred_element_type=jnp.float32
            )
            if part < PARTS:
                x_out[queries_here, at] = terms.astype(x_out.dtype)
            else:
                own_terms[queries_here, at] = terms
            if 1 <= part <= PARTS:
                x_copy(step, part - 1).start()

        if step > 0:
            finish(step - 1)

    for step in range(STEPS):
        one_step(step)
    finish(STEPS - 1)

    for step in range(STEPS):
        for part in range(PARTS):
            x_copy(step, part).wait_send()
    for copy in c_copies(sub):
        copy.wait_send()
    w_copy(sub).wait_send()

    @pl.when(has_z)
    def _():
        for step in range(STEPS):
            for copy in z_copies(step, sub):
                copy.wait_send()


def local(queries, keys, values, half_width, valid_length, out_weight):
    rows, width = queries.shape
    bf16 = jnp.bfloat16
    dma = pltpu.SemaphoreType.DMA
    return pl.pallas_call(
        kernel,
        out_shape=jax.ShapeDtypeStruct((rows, width), bf16),
        in_specs=[pl.BlockSpec(memory_space=pltpu.SMEM)] * 2
        + [pl.BlockSpec(memory_space=pl.ANY)] * 4,
        out_specs=pl.BlockSpec(memory_space=pltpu.VMEM),
        scratch_shapes=[
            pltpu.VMEM((rows, width), bf16),
            pltpu.VMEM((3 * rows, width), bf16),
            pltpu.VMEM((3 * rows, width), bf16),
            pltpu.VMEM((2,) + out_weight.shape, bf16),
            pltpu.VMEM((REACH, 2 * rows + REACH), jnp.int32),
            pltpu.VMEM((REACH, width), bf16),
            pltpu.VMEM((rows, width), jnp.float32),
            pltpu.VMEM((rows, width), bf16),
            pltpu.VMEM((rows, width), bf16),
            dma((4,)),
            dma((2, STEPS)),
            dma((2, STEPS)),
            dma((2,)),
            dma((2,)),
            dma,
            dma,
            dma((STEPS, PARTS)),
            dma((STEPS, PARTS)),
        ],
        compiler_params=pltpu.CompilerParams(
            collective_id=0, has_side_effects=True, vmem_limit_bytes=60 << 20
        ),
    )(half_width, valid_length, queries, keys, values, out_weight)


def solution(mesh):
    placed = (
        P(("parts", "seq", "sub"), "heads"),
        P(("parts", "seq", "sub"), "heads"),
        P(("parts", "seq", "sub"), "heads"),
        P(),
        P("parts"),
        P("heads", "sub"),
    )
    return jax.shard_map(
        local,
        mesh=mesh,
        in_specs=placed,
        out_specs=P(("parts", "seq", "sub"), "heads"),
        check_vma=False,
    )
```
